32 devices in a mesh: wide: 8 (over y, x, core), blk: 4 (over z).
Axes of the slice: x: 2, y: 2, z: 4, core: 2. Of those that a mesh axis runs over, the one named last changes fastest.
Arguments:
- visual_features: bfloat16 [32768, 1152], P(('wide', 'blk')), may hold values from -0.1875 to 0.1875
- sentence_features: bfloat16 [1024, 1152], P(('wide', 'blk')), may hold values from -0.1875 to 0.1875
- true_partner_ids: int32 [32768], P(('wide', 'blk')), may hold values from 0 to 1023
- inverse_warmth: float32 [], replicated, may hold values from 90 to 110
- additive_adjust: float32 [], replicated, may hold values from -12 to -9
Outputs:
- grad_images: float32 [32768, 1152], P(('wide', 'blk'))
- grad_texts: float32 [1024, 1152], P(('wide', 'blk'))
The draws below stay inside these ranges and needn't reach their ends.
Inputs may be any that keep to these rules, and one draw needn't show every extreme that they name: Image i is paired with text true_partner_ids[i]; a text may be paired with several images or none.
All inputs are finite; a program needn't handle non-finite values.
Results may differ from the reference program's by a relative error of at most 0.007.
Values may be sent and summed in bfloat16 or wider, within the bound.
No kernel may reach another device: no remote copies, remote signals or barrier semaphores. Data moves between devices by JAX's collectives and lax.ppermute only.
A program may use at most 64 MiB of HBM per device.

```python
import jax
import jax.numpy as jnp
from jax import lax

D = 1152
IMG_DEV = 1024
IMAGES = 32768
TEXTS = 1024


def with_ends(array, rng, smallest, high):
    longest = array.shape.index(max(array.shape))
    spots = []
    for shift in (0, 1):
        where = [jax.random.randint(jax.random.fold_in(rng, axis), (), 0, length) for axis, length in enumerate(array.shape)]
        where[longest] = (where[longest] + shift) % array.shape[longest]
        spots.append(tuple(where))
    return array.at[spots[0]].set(smallest).at[spots[1]].set(high)


def steps_of(stream_key, shape, cuts, least, largest):
    gain, own = 1.0, jax.random.fold_in(stream_key, 6)
    for axis_at, shards_of in cuts:
        draws = jnp.exp(jax.random.uniform(jax.random.fold_in(own, axis_at), (shards_of,), jnp.float32, least / len(cuts), largest / len(cuts)))
        gain = gain * jnp.repeat(draws, shape[axis_at] // shards_of).reshape([-1 if axis == axis_at else 1 for axis in range(len(shape))])
    return gain


def scatter_about(key, shape, width, bound, shards=(), kind=jnp.bfloat16):
    gain = steps_of(key, shape, shards, -0.22, 0.18) if shards else 1.0
    values = jax.random.normal(key, shape, jnp.float32) * width * gain
    return jnp.minimum(jnp.maximum(values, -bound), bound).astype(kind)


def setup_inputs(seed: int = 0) -> dict:
    arg_keys = jax.random.split(jax.random.key(seed), 6)
    return {
        "visual_features": scatter_about(arg_keys[0], (IMAGES, D), D ** -0.5, 0.1875, ((0, 32),)),
        "sentence_features": scatter_about(arg_keys[1], (TEXTS, D), D ** -0.5, 0.1875, ((0, 32),)),
        "true_partner_ids": with_ends(jax.random.randint(arg_keys[2], (IMAGES,), 0, TEXTS), jax.random.fold_in(arg_keys[2], 1), 0, TEXTS - 1).astype(jnp.int32),
        "inverse_warmth": jnp.clip(jax.random.uniform(arg_keys[3], (), jnp.float32, 90.0, 110.0), 90.0, 110.0),
        "additive_adjust": jnp.clip(jax.random.uniform(arg_keys[4], (), jnp.float32, -12.0, -9.0), -12.0, -9.0),
    }


def piecewise_updates(visual_part, aligned_text_part, sentence_features, inverse_warmth, additive_adjust):
    cosine_grid = jnp.dot(visual_part, sentence_features.T, preferred_element_type=jnp.float32)
    sigmoid_levels = inverse_warmth * cosine_grid + additive_adjust
    columns = jnp.arange(sentence_features.shape[0], dtype=jnp.int32)
    plus_minus_ones = jnp.where(aligned_text_part[:, None] == columns[None, :], 1.0, -1.0).astype(sigmoid_levels.dtype)
    loss_grid_scaled = (-inverse_warmth * plus_minus_ones * jax.nn.sigmoid(-plus_minus_ones * sigmoid_levels)).astype(jnp.bfloat16)
    incoming_grad_part = jnp.dot(loss_grid_scaled, sentence_features, preferred_element_type=jnp.float32)
    returned_grad_part = jnp.dot(loss_grid_scaled.T, visual_part, preferred_element_type=jnp.float32)
    return incoming_grad_part, returned_grad_part


def reference(visual_features, sentence_features, true_partner_ids, inverse_warmth, additive_adjust):
    count = visual_features.shape[0] // IMG_DEV
    img_blocks = visual_features.reshape(count, IMG_DEV, visual_features.shape[1])
    pair_blocks = true_partner_ids.reshape(count, IMG_DEV)

    def scan_step(carry, running_dot_sums):
        incoming_grad_part, returned_grad_part = piecewise_updates(running_dot_sums[0], running_dot_sums[1], sentence_features, inverse_warmth, additive_adjust)
        return carry + returned_grad_part, incoming_grad_part

    start = jnp.zeros(sentence_features.shape, jnp.float32)
    grad_texts, grad_blocks = lax.scan(scan_step, start, (img_blocks, pair_blocks))
    grad_images = grad_blocks.reshape(visual_features.shape)
    return grad_images, grad_texts
```

```python
import functools

import jax
import jax.numpy as jnp
import numpy as np
from jax import lax
from jax.experimental import pallas as pl
from jax.experimental.pallas import tpu as pltpu
from jax.sharding import PartitionSpec as P

F32, BF16 = jnp.float32, jnp.bfloat16
ROWS, LANES = (((0,), (0,)), ((), ())), (((1,), (1,)), ((), ()))


def weight_block(texts, images, columns, partners, scale, bias):
    scores = lax.dot_general(texts, images, LANES, preferred_element_type=F32)
    logits = scale * scores + bias
    paired = columns == partners
    margin = jnp.where(paired, logits, -logits)
    factor = jnp.where(paired, -scale, scale)
    return (factor / (1.0 + jnp.exp(margin))).astype(BF16)


def weights_kernel(
    half, scale_ref, bias_ref, own_ref, other_ref, own_ids, other_ids, columns_ref, near_ref, far_ref,
    own_w, other_w, near_out, far_out, texts, total,
):
    step = pl.program_id(0)
    rows = near_ref.shape[0]

    @pl.when(step == 0)
    def _():
        texts[:rows] = near_ref[...]
        texts[rows:] = far_ref[...]
        total[...] = jnp.zeros_like(total)

    def block(images_ref, ids_ref, w_ref):
        w = weight_block(
            texts[...], images_ref[...], columns_ref[...], ids_ref[...], scale_ref[0], bias_ref[0]
        )
        w_ref[...] = w
        total[...] += jnp.dot(w, images_ref[...], preferred_element_type=F32)

    @pl.when(step < half)
    def _():
        block(own_ref, own_ids, own_w)

    @pl.when(step >= half)
    def _():
        block(other_ref, other_ids, other_w)

    @pl.when(step == pl.num_programs(0) - 1)
    def _():
        near_out[...] = total[:rows].astype(near_out.dtype)
        far_out[...] = total[rows:].astype(far_out.dtype)


def weights_and_texts(scale, bias, images, ids, columns, near, far, near_type):
    count, width = images[0].shape
    rows = near.shape[0]
    block = min(count, 512)
    half = count // block
    first = lambda i: jnp.minimum(i, half - 1)
    second = lambda i: jnp.maximum(i - half, 0)
    smem = pl.BlockSpec(memory_space=pltpu.SMEM)
    whole = lambda shape: pl.BlockSpec(shape, lambda i: (0, 0))
    return pl.pallas_call(
        functools.partial(weights_kernel, half),
        grid=(2 * half,),
        in_specs=[
            smem,
            smem,
            pl.BlockSpec((block, width), lambda i: (first(i), 0)),
            pl.BlockSpec((block, width), lambda i: (second(i), 0)),
            pl.BlockSpec((1, block), lambda i: (0, first(i))),
            pl.BlockSpec((1, block), lambda i: (0, second(i))),
            whole((2 * rows, 1)),
            whole((rows, width)),
            whole((rows, width)),
        ],
        out_specs=[
            pl.BlockSpec((2 * rows, block), lambda i: (0, first(i))),
            pl.BlockSpec((2 * rows, block), lambda i: (0, second(i))),
            whole((rows, width)),
            whole((rows, width)),
        ],
        out_shape=[
            jax.ShapeDtypeStruct((2 * rows, count), BF16),
            jax.ShapeDtypeStruct((2 * rows, count), BF16),
            jax.ShapeDtypeStruct((rows, width), near_type),
            jax.ShapeDtypeStruct((rows, width), BF16),
        ],
        scratch_shapes=[pltpu.VMEM((2 * rows, width), BF16), pltpu.VMEM((2 * rows, width), F32)],
        cost_estimate=pl.CostEstimate(
            flops=16 * rows * count * width,
            transcendentals=4 * rows * count,
            bytes_accessed=4 * count * width + 16 * rows * count,
        ),
    )(scale, bias, *images, *ids, columns, near, far)


def images_kernel(pieces, *refs):
    weights, texts, out = refs[: len(pieces)], refs[len(pieces) : -1], refs[-1]
    total, at = None, 0
    for w, parts in zip(weights, pieces):
        row = 0
        for _ in range(parts):
            text = texts[at]
            at += 1
            rows = text.shape[0]
            term = lax.dot_general(
                w[row : row + rows, :], text[...], ROWS, preferred_element_type=F32
            )
            total = term if total is None else total + term
            row += rows
    out[...] = total


def image_grads(weights, texts):
    count, width = weights[0].shape[1], texts[0][0].shape[1]
    block = min(count, 256)
    flat = [piece for group in texts for piece in group]
    rows = sum(piece.shape[0] for piece in flat)
    return pl.pallas_call(
        functools.partial(images_kernel, [len(group) for group in texts]),
        grid=(count // block,),
        in_specs=[pl.BlockSpec((w.shape[0], block), lambda i: (0, i)) for w in weights]
        + [pl.BlockSpec(piece.shape, lambda i: (0, 0)) for piece in flat],
        out_specs=pl.BlockSpec((block, width), lambda i: (i, 0)),
        out_shape=jax.ShapeDtypeStruct((count, width), F32),
        cost_estimate=pl.CostEstimate(
            flops=2 * rows * count * width,
            transcendentals=0,
            bytes_accessed=2 * rows * count + 4 * count * width,
        ),
    )(*weights, *flat)


def shards(wide, blk, images, texts, ids, scale, bias):
    rows, width = texts.shape
    plane = wide // 2

    def swap(array, axis, size, mask):
        return lax.ppermute(array, axis, [(i, i ^ mask) for i in range(size)])

    pair = lambda array: swap(array, "wide", wide, 1)
    across = lambda array, mask: swap(array, "wide", wide, 2 * mask)
    along = lambda array, mask: swap(array, "blk", blk, mask)

    scale, bias = scale.reshape(1), bias.reshape(1)
    ids = ids.reshape(1, -1)
    lines = [texts] + [along(texts, mask) for mask in range(1, blk)]
    both_images = (images, pair(images))
    both_ids = (ids, pair(ids))
    line = jnp.concatenate(lines)

    masks, places = np.meshgrid(np.arange(plane), np.arange(blk), indexing="ij")
    owner = (lax.axis_index("wide") ^ (2 * masks)) * blk + (lax.axis_index("blk") ^ places)
    columns = (owner[:, :, None] * rows + np.arange(rows)).reshape(plane, blk * rows, 1)

    groups = [line] + [across(line, mask) for mask in range(1, plane)]
    weights, grads, ours, theirs, their_texts = [], [], [], [], []
    for at in range(0, plane, 2):
        own_w, other_w, near, far = weights_and_texts(
            scale, bias, both_images, both_ids, columns[at : at + 2].reshape(-1, 1),
            groups[at], groups[at + 1], F32 if at == 0 else BF16,
        )
        grads += [near, far]
        ours.append(own_w)
        theirs.append(pair(other_w))
        their_texts.append([pair(groups[at]), pair(groups[at + 1])])

    mine = grads[0]
    for mask in range(1, plane):
        mine = mine + across(grads[mask], mask).astype(F32)
    parts = mine.reshape(blk, rows, width)
    grad_texts = parts[0]
    for mask in range(1, blk):
        grad_texts = grad_texts + along(parts[mask].astype(BF16), mask).astype(F32)

    our_texts = [[groups[at], groups[at + 1]] for at in range(0, plane, 2)]
    grad_images = image_grads(ours + theirs, our_texts + their_texts)
    return grad_images, grad_texts


def solution(mesh):
    wide, blk = mesh.shape["wide"], mesh.shape["blk"]
    both = P(("wide", "blk"), None)
    return jax.shard_map(
        functools.partial(shards, wide, blk),
        mesh=mesh,
        in_specs=(both, both, P(("wide", "blk")), P(), P()),
        out_specs=(both, both),
        check_vma=False,
    )
```
